128 devices in a mesh: dp: 32 (over y, x, core), vocab: 4 (over z).
Axes of the slice: x: 4, y: 4, z: 4, core: 2. Of those that a mesh axis runs over, the one named last changes fastest.
Arguments:
- resid: bfloat16 [2, 4096, 4096], P(None, 'dp'), may hold values from -6 to 6
- norm_gain: float32 [4096], replicated, may hold values from 0.5 to 1.5
- in_x: bfloat16 [4096, 4096], P('dp', 'vocab'), may hold values from -0.09375 to 0.09375
- in_z: bfloat16 [4096, 4096], P('dp', 'vocab'), may hold values from -0.09375 to 0.09375
- conv_w: float32 [4, 4096], P(None, 'vocab'), may hold values from -3 to 3
- conv_b: float32 [4096], P('vocab'), may hold values from -3 to 3
- xdt_w: bfloat16 [4096, 256], P('vocab'), may hold values from -0.09375 to 0.09375
- xbc_w: bfloat16 [4096, 32], P('vocab'), may hold values from -0.09375 to 0.09375
- dt_gain: float32 [256], replicated, may hold values from 0.5 to 1.5
- dt_proj: bfloat16 [256, 4096], P(None, 'vocab'), may hold values from -0.375 to 0.375
- dt_bias: float32 [4096], P('vocab'), may hold values from -4 to 1
- a_rate: float32 [4096, 16], P('vocab'), may hold values from 0.0001 to 1
- out_w: bfloat16 [4096, 4096], P('vocab'), may hold values from -0.09375 to 0.09375
- final_gain: float32 [4096], replicated, may hold values from 0.5 to 1.5
- head_w: bfloat16 [8192, 4096], P('vocab', 'dp'), as said below
- targets: int32 [2, 4096], P(None, 'dp'), may hold values from 0 to 8191
- lengths: int32 [2], replicated, may hold values from 1024 to 4096
Outputs:
- hidden_out: bfloat16 [2, 4096, 4096], P(None, 'dp', 'vocab')
- token_logp: float32 [2, 4096], P(None, 'dp')
- mean_logp: float32 [], replicated
The draws below stay inside these ranges and needn't reach their ends.
Inputs may be any that keep to these rules, and one draw needn't show every extreme that they name: `head_w`: entries lie within 720 / sqrt(4096) of zero.
All inputs are finite; a program needn't handle non-finite values.
Results may differ from the reference program's by a relative error of at most 0.019.
Values may be sent and summed in bfloat16 or wider, within the bound.
No kernel may reach another device: no remote copies, remote signals or barrier semaphores. Data moves between devices by JAX's collectives and lax.ppermute only.
A program may use at most 128 MiB of HBM per device.

```python
import math
import jax
import jax.numpy as jnp
from jax import lax

D = 4096
N = 16
R = 256
KCONV = 4
B = 2
L = 4096
E = 4096
V = 8192


def draw_head_w(key, part):
    values = jnp.clip(jax.random.normal(key, (V, D), jnp.float32), -6.0, 6.0) * (3.0 / math.sqrt(D))
    return values.astype(jnp.bfloat16)


def plant(entries, key, least, largest):
    spot = [jax.random.randint(jax.random.fold_in(key, axis), (), 0, length) for axis, length in enumerate(entries.shape)]
    main_axis = entries.shape.index(max(entries.shape))
    beside = spot[:main_axis] + [(spot[main_axis] + 1) % entries.shape[main_axis]] + spot[main_axis + 1:]
    return entries.at[tuple(spot)].set(least).at[tuple(beside)].set(largest)


def steps_of(key, extent, shards, low, largest):
    loudness, own = 1.0, jax.random.fold_in(key, 6)
    for position, shards_of in shards:
        steps = jnp.exp(jax.random.uniform(jax.random.fold_in(own, position), (shards_of,), jnp.float32, low / len(shards), largest / len(shards)))
        loudness = loudness * jnp.repeat(steps, extent[position] // shards_of).reshape([-1 if axis == position else 1 for axis in range(len(extent))])
    return loudness


def normal_values(key, extent, width, most, split=(), kind=jnp.bfloat16):
    array = jax.random.normal(key, extent, jnp.float32) * width
    if len(split) > 0:
        array = steps_of(key, extent, split, -0.22, 0.18) * array
    return jnp.clip(array, min=-most, max=most).astype(kind)


def setup_inputs(seed: int = 0) -> dict:
    keys = jax.random.split(jax.random.key(seed), 18)
    return {
        "resid": normal_values(keys[0], (B, L, D), 1.0, 6.0, ((1, 32),)),
        "norm_gain": jnp.clip(1.0 + 0.1 * jax.random.normal(keys[1], (D,), jnp.float32), 0.5, 1.5),
        "in_x": normal_values(keys[2], (D, E), D ** -0.5, 0.09375, ((0, 32), (1, 4))),
        "in_z": normal_values(keys[3], (D, E), D ** -0.5, 0.09375, ((0, 32), (1, 4))),
        "conv_w": normal_values(keys[4], (KCONV, E), 0.5, 3.0, ((1, 4),), jnp.float32),
        "conv_b": normal_values(keys[5], (E,), 0.5, 3.0, ((0, 4),), jnp.float32),
        "xdt_w": normal_values(keys[6], (E, R), E ** -0.5, 0.09375, ((0, 4),)),
        "xbc_w": normal_values(keys[7], (E, 2 * N), E ** -0.5, 0.09375, ((0, 4),)),
        "dt_gain": jnp.clip(1.0 + 0.1 * jax.random.normal(keys[8], (R,), jnp.float32), 0.5, 1.5),
        "dt_proj": normal_values(keys[9], (R, E), R ** -0.5, 0.375, ((1, 4),)),
        "dt_bias": jnp.clip(-4.0 + 5.0 * jax.random.uniform(keys[10], (E,), jnp.float32) ** steps_of(keys[10], (E,), ((0, 4),), -0.2, 0.2), -4.0, 1.0),
        "a_rate": jnp.clip(jnp.exp(math.log(1.0) - 9.2103404 * jax.random.uniform(keys[11], (E, N), jnp.float32) ** steps_of(keys[11], (E, N), ((0, 4),), -0.2, 0.2)), 0.0001, 1.0),
        "out_w": normal_values(keys[12], (E, D), E ** -0.5, 0.09375, ((0, 4),)),
        "final_gain": jnp.clip(1.0 + 0.1 * jax.random.normal(keys[13], (D,), jnp.float32), 0.5, 1.5),
        "head_w": draw_head_w(jax.random.fold_in(keys[17], 71), 0),
        "targets": plant(jax.random.randint(keys[15], (B, L), 0, V), jax.random.fold_in(keys[15], 1), 0, V - 1).astype(jnp.int32),
        "lengths": jax.random.randint(keys[16], (B,), L // 4, L + 1).astype(jnp.int32),
    }


def rms_norm(values, gain, epsilon):
    return values * lax.rsqrt(lax.optimization_barrier(jnp.mean(values * values, axis=-1, keepdims=True)) + epsilon) * gain

def reference(resid, norm_gain, in_x, in_z, conv_w, conv_b, xdt_w, xbc_w, dt_gain, dt_proj, dt_bias, a_rate, out_w, final_gain, head_w, targets, lengths):
    stream = resid.astype(jnp.float32)
    normed = rms_norm(stream, norm_gain, 1e-05).astype(jnp.bfloat16).reshape(B * L, D)
    x_inner = jnp.dot(normed, in_x, preferred_element_type=jnp.float32).astype(jnp.bfloat16).reshape(B, L, E)
    z_gate = jnp.dot(normed, in_z, preferred_element_type=jnp.float32).astype(jnp.bfloat16).reshape(B, L, E)
    padded = jnp.pad(x_inner.astype(jnp.float32), ((0, 0), (KCONV - 1, 0), (0, 0)))
    conv_sum = jnp.zeros((B, L, E), jnp.float32) + conv_b
    for tap_index in range(KCONV):
        conv_sum = conv_sum + conv_w[tap_index] * padded[:, tap_index:tap_index + L, :]
    conv_act = jax.nn.silu(conv_sum)
    conv_low = conv_act.astype(jnp.bfloat16).reshape(B * L, E)
    dt_raw = jnp.dot(conv_low, xdt_w, preferred_element_type=jnp.float32)
    bc_raw = jnp.dot(conv_low, xbc_w, preferred_element_type=jnp.float32)
    dt_normed = rms_norm(dt_raw, dt_gain, 1e-06).astype(jnp.bfloat16)
    step_size = jax.nn.softplus(jnp.dot(dt_normed, dt_proj, preferred_element_type=jnp.float32) + dt_bias).reshape(B, L, E)
    in_map = bc_raw[:, :N].reshape(B, L, N)
    out_map = bc_raw[:, N:].reshape(B, L, N)

    def advance(carry_state, inputs):
        step_now, conv_now, in_now, out_now = inputs
        carry_state = jnp.exp(-step_now[..., None] * a_rate) * carry_state + (step_now * conv_now)[..., None] * in_now[:, None, :]
        return (carry_state, lax.optimization_barrier(jnp.sum(carry_state * out_now[:, None, :], axis=-1)))
    start_state = jnp.zeros((B, E, N), jnp.float32)
    inputs = (step_size.transpose(1, 0, 2), conv_act.transpose(1, 0, 2), in_map.transpose(1, 0, 2), out_map.transpose(1, 0, 2))
    _, scanned = lax.scan(advance, start_state, inputs)
    mixed = scanned.transpose(1, 0, 2)
    gated = (mixed * jax.nn.silu(z_gate.astype(jnp.float32))).astype(jnp.bfloat16).reshape(B * L, E)
    mixer_out = jnp.dot(gated, out_w, preferred_element_type=jnp.float32)
    hidden = (stream.reshape(B * L, D) + mixer_out).astype(jnp.bfloat16)
    final = rms_norm(hidden.astype(jnp.float32), final_gain, 1e-05).astype(jnp.bfloat16)
    logits = lax.dot_general(final, head_w, (((1,), (1,)), ((), ())), preferred_element_type=jnp.float32)
    row_top = lax.optimization_barrier(jnp.max(logits, axis=-1))
    log_total = row_top + jnp.log(lax.optimization_barrier(jnp.sum(jnp.exp(logits - row_top[:, None]), axis=-1)))
    picked = jnp.take_along_axis(logits, targets.reshape(B * L, 1).astype(jnp.int32), axis=1)[:, 0]
    token_logp = (picked - log_total).reshape(B, L)
    valid_mask = jnp.arange(L, dtype=jnp.int32)[None, :] < lengths[:, None]
    mean_logp = jnp.sum(jnp.where(valid_mask, token_logp, 0.0)) / jnp.sum(lengths.astype(jnp.float32))
    return (hidden.reshape(B, L, D), token_logp, mean_logp)
```

```python
import math

import jax
import jax.numpy as jnp
from jax import lax
from jax.experimental import pallas as pl
from jax.experimental.pallas import tpu as pltpu
from jax.sharding import Mesh
from jax.sharding import PartitionSpec as P

DP = ("dp_0", "dp_1", "dp_2")
CHIPS = ("dp_0", "dp_1")
YS, XS, CS = 4, 4, 2
BF = jnp.bfloat16
F32 = jnp.float32
LOG2E = math.log2(math.e)


def place(y, x, c):
    return ((y % YS) * XS + x % XS) * CS + c


def turns(by, phase):
    pairs = []
    for y in range(YS):
        for x in range(XS):
            for c in range(CS):
                along_x = (c == 0) == (phase == 0)
                to = place(y, x + by, c) if along_x else place(y + by, x, c)
                pairs.append((place(y, x, c), to))
    return pairs


def ring(peers, by):
    return [(i, (i + by) % peers) for i in range(peers)]


def swap_cores(array):
    return lax.ppermute(array, "dp_2", ring(CS, 1))


def line_of_chips(shard):
    near = {s: lax.ppermute(shard, DP, turns(s, 0)) for s in (1, 3, 2)}
    return jnp.concatenate([shard, near[1], near[2], near[3]], axis=0)


def blocks_in_order(y, x, core):
    found = []
    for s2 in range(4):
        for s1 in range(4):
            first = lax.rem(y - s2 + YS, YS) * XS + lax.rem(x - s1 + XS, XS)
            second = lax.rem(y - s1 + YS, YS) * XS + lax.rem(x - s2 + XS, XS)
            found.append(jnp.where(core == 0, first, second) * CS + core)
    return found


def rms_norm(values, gain, epsilon):
    return values * lax.rsqrt(jnp.mean(values * values, axis=-1, keepdims=True) + epsilon) * gain


def dot(a, b):
    return jnp.dot(a, b, preferred_element_type=F32)


def norm_kernel(wide, order, resid, tail, gain, normed, mine, theirs, tail_normed):
    rows, halo = resid.shape[0], tail.shape[0]
    for r in range(0, rows, 32):
        normed[r : r + 32] = rms_norm(resid[r : r + 32].astype(F32), gain[...], 1e-05).astype(BF)
    tail_normed[...] = rms_norm(tail[...].astype(F32), gain[...], 1e-05).astype(BF)
    count = mine.shape[1] // wide
    for k in range(2 * count):
        out = (mine, theirs)[k // count]
        at = pl.ds(pl.multiple_of(order[k] * wide, wide), wide)
        to = slice((k % count) * wide, (k % count + 1) * wide)
        out[:rows, to] = normed[:, at]
        out[rows : rows + halo, to] = tail_normed[:, at]


def steps_kernel(rows, length, nstate, bc, dt, gain, proj, bias, conv, rate, step3, du3, last, total):
    raw = dt[...]
    normed = rms_norm(raw, gain[...], 1e-06).astype(BF)
    v = dot(normed, proj[...]) + bias[...]
    step = jnp.maximum(v, 0.0) + jnp.log1p(jnp.exp(-jnp.abs(v)))
    du = step * conv[...]
    for j in range(step3.shape[1]):
        step3[:, j, :] = step[:, j * 128 : (j + 1) * 128]
        du3[:, j, :] = du[:, j * 128 : (j + 1) * 128]
    batches = rows // length

    def advance(t, carry):
        state, sums = carry
        state, sums = list(state), list(sums)
        for b in range(batches):
            at = b * length + t
            s, u = step3[at], du3[at]
            sums[b] = sums[b] + s
            for n in range(nstate):
                k = b * nstate + n
                state[k] = jnp.exp2(s * rate[n]) * state[k] + u * bc[at * 2 * nstate + n]
        return tuple(state), tuple(sums)

    zero = jnp.zeros(step3.shape[1:], F32)
    state, sums = lax.fori_loop(
        0, length, advance, ((zero,) * (batches * nstate), (zero,) * batches), unroll=2
    )
    for b in range(batches):
        total[b] = sums[b]
        for n in range(nstate):
            last[b, n] = state[b * nstate + n]


def outputs_kernel(rows, length, nstate, bc, step3, du3, rate, start, z, gated, y3):
    batches = rows // length

    def advance(t, state):
        state = list(state)
        for b in range(batches):
            at = b * length + t
            s, u = step3[at], du3[at]
            y = None
            for n in range(nstate):
                k = b * nstate + n
                state[k] = jnp.exp2(s * rate[n]) * state[k] + u * bc[at * 2 * nstate + n]
                part = state[k] * bc[at * 2 * nstate + nstate + n]
                y = part if y is None else y + part
            y3[at] = y
        return tuple(state)

    state = tuple(start[b, n] for b in range(batches) for n in range(nstate))
    lax.fori_loop(0, length, advance, state, unroll=2)
    for j in range(y3.shape[1]):
        gate = z[:, j * 128 : (j + 1) * 128].astype(F32)
        gate = gate / (1.0 + jnp.exp(-gate))
        gated[:, j * 128 : (j + 1) * 128] = (y3[:, j, :] * gate).astype(BF)


def vmem():
    return pl.BlockSpec(memory_space=pltpu.VMEM)


def smem():
    return pl.BlockSpec(memory_space=pltpu.SMEM)


def body(
    resid,
    norm_gain,
    in_x,
    in_z,
    conv_w,
    conv_b,
    xdt_w,
    xbc_w,
    dt_gain,
    dt_proj,
    dt_bias,
    a_rate,
    out_w,
    final_gain,
    head_w,
    targets,
    lengths,
):
    batch_count, local_len, width = resid.shape
    k_rows, channels = in_x.shape
    nstate = a_rate.shape[1]
    taps = conv_w.shape[0]
    rank = xdt_w.shape[1]
    rows = batch_count * local_len
    y, x, core = (lax.axis_index(a) for a in DP)
    zi = lax.axis_index("vocab")
    zs = lax.axis_size("vocab")

    all_z = lax.all_gather(in_z, DP, axis=0, tiled=True)

    order = [(i, i + 1) for i in range(YS * XS * CS - 1)]
    tail = lax.ppermute(resid[:, local_len - (taps - 1) :, :], DP, order)
    line = line_of_chips(in_x)
    far = {s: lax.ppermute(line, DP, turns(s, 1)) for s in (1, 3, 2)}
    pieces = [line] + [far[s] for s in (1, 2, 3)]
    halo = 16
    tail = jnp.pad(
        tail.reshape(batch_count * (taps - 1), width),
        ((0, halo - batch_count * (taps - 1)), (0, 0)),
    )
    tail, _ = lax.optimization_barrier((tail, line))
    flat = resid.reshape(rows, width)
    half_rows = jax.ShapeDtypeStruct((rows + halo, width // CS), BF)
    normed, mine, theirs = pl.pallas_call(
        lambda *refs: norm_kernel(k_rows, *refs),
        out_shape=(jax.ShapeDtypeStruct((rows, width), BF), half_rows, half_rows),
        in_specs=[smem()] + [vmem()] * 3,
        out_specs=(vmem(),) * 3,
        scratch_shapes=[pltpu.VMEM((halo, width), BF)],
        compiler_params=pltpu.CompilerParams(vmem_limit_bytes=48 << 20),
        name="norm",
    )(
        jnp.stack(blocks_in_order(y, x, core) + blocks_in_order(y, x, 1 - core)),
        flat,
        tail,
        norm_gain.reshape(1, width),
    )
    theirs = swap_cores(theirs)
    depth = width // CS // 4
    cut = [slice(s * depth, (s + 1) * depth) for s in range(4)]
    turn = (0, 1, 3, 2)
    for_them = sum(dot(theirs[:, cut[s]], pieces[s]) for s in turn)
    from_them = swap_cores(for_them.astype(BF))
    x_acc = sum(dot(mine[:, cut[s]], pieces[s]) for s in turn) + from_them.astype(F32)
    x_all = x_acc.astype(BF)
    x_inner = x_all[:rows].reshape(batch_count, local_len, channels)
    before = x_all[rows : rows + batch_count * (taps - 1)].reshape(batch_count, taps - 1, channels)
    padded = jnp.concatenate([before, x_inner], axis=1).astype(F32)
    conv_sum = jnp.zeros((batch_count, local_len, channels), F32) + conv_b
    for k in range(taps):
        conv_sum = conv_sum + conv_w[k] * padded[:, k : k + local_len, :]
    conv_act = jax.nn.silu(conv_sum).reshape(rows, channels)
    low = dot(conv_act.astype(BF), jnp.concatenate([xdt_w, xbc_w], axis=1))
    low_sent = low.astype(BF)
    low_sum = low_sent.astype(F32)
    for s in (1, 3, 2):
        low_sum = low_sum + lax.ppermute(low_sent, "vocab", ring(zs, s)).astype(F32)
    head_t, _, _ = lax.optimization_barrier((head_w.T, all_z, low_sum))
    all_head = lax.all_gather(head_t, DP, axis=0, tiled=True)
    dt_raw = low_sum[:, :rank]
    bc_raw = low_sum[:, rank:].reshape(-1)

    fold = channels // 128
    rate = (a_rate.T * (-LOG2E)).reshape(nstate, fold, 128)
    seq = jax.ShapeDtypeStruct((rows, fold, 128), F32)
    step3, du3, last, total = pl.pallas_call(
        lambda *refs: steps_kernel(rows, local_len, nstate, *refs),
        out_shape=(
            seq,
            seq,
            jax.ShapeDtypeStruct((batch_count, nstate, fold, 128), F32),
            jax.ShapeDtypeStruct((batch_count, fold, 128), F32),
        ),
        in_specs=[smem()] + [vmem()] * 6,
        out_specs=(vmem(),) * 4,
        compiler_params=pltpu.CompilerParams(vmem_limit_bytes=48 << 20),
        name="steps",
    )(
        bc_raw,
        dt_raw,
        dt_gain.reshape(1, rank),
        dt_proj,
        dt_bias.reshape(1, channels),
        conv_act,
        rate,
    )

    half = nstate // CS
    own = lax.dynamic_slice_in_dim(last, core * half, half, 1)
    other = lax.dynamic_slice_in_dim(last, (1 - core) * half, half, 1)
    rate_half = lax.dynamic_slice_in_dim(rate, core * half, half, 0)
    sent = jnp.concatenate([other, total[:, None]], axis=1)
    got = swap_cores(sent)
    state_0 = jnp.where(core == 0, own, got[:, :half])
    state_1 = jnp.where(core == 0, got[:, :half], own)
    total_0 = jnp.where(core == 0, total, got[:, half])
    total_1 = jnp.where(core == 0, got[:, half], total)

    def decay(steps):
        return jnp.exp2(steps[:, None] * rate_half)

    chip_state = decay(total_1) * state_0 + state_1
    chip_total = total_0 + total_1
    coarse = chip_total.astype(BF)
    fine = (chip_total - coarse.astype(F32)).astype(BF)
    packed = jnp.concatenate(
        [chip_state.astype(BF), coarse[:, None], fine[:, None]], axis=1
    )
    chips = YS * XS
    everyone = lax.all_to_all(
        jnp.broadcast_to(packed[None], (chips, *packed.shape)), CHIPS, 0, 0, tiled=True
    )
    z_gate = dot(normed, all_z).astype(BF)
    everyone, z_gate = lax.optimization_barrier((everyone, z_gate))
    chip = y * XS + x
    enter = jnp.zeros_like(chip_state)
    for k in range(chips - 1):
        part = everyone[k].astype(F32)
        later = decay(part[:, half] + part[:, half + 1]) * enter + part[:, :half]
        enter = jnp.where(k < chip, later, enter)
    enter_1 = decay(total_0) * enter + state_0
    kept = jnp.where(core == 0, enter, enter_1)
    given = swap_cores(jnp.where(core == 0, enter_1, enter))
    start = jnp.concatenate(
        [jnp.where(core == 0, kept, given), jnp.where(core == 0, given, kept)], axis=1
    )

    gated = pl.pallas_call(
        lambda *refs: outputs_kernel(rows, local_len, nstate, *refs),
        out_shape=jax.ShapeDtypeStruct((rows, channels), BF),
        in_specs=[smem()] + [vmem()] * 5,
        out_specs=vmem(),
        scratch_shapes=[pltpu.VMEM((rows, fold, 128), F32)],
        compiler_params=pltpu.CompilerParams(vmem_limit_bytes=48 << 20),
        name="outputs",
    )(bc_raw, step3, du3, rate, start, z_gate)

    share = width // zs

    def out_share(by):
        to = lax.rem(zi + by, zs) * share
        return dot(gated, lax.dynamic_slice_in_dim(out_w, to, share, 1))

    arrived = [lax.ppermute(out_share(s).astype(BF), "vocab", ring(zs, s)) for s in (1, 3, 2)]
    mixer = out_share(0)
    for piece in arrived:
        mixer = mixer + piece.astype(F32)
    part = lax.dynamic_slice_in_dim(flat, zi * share, share, 1).astype(F32)
    hidden_share = (part + mixer).astype(BF)
    hidden = jnp.zeros((rows, width), BF)
    for s in (0, 1, 3, 2):
        piece = hidden_share if s == 0 else lax.ppermute(hidden_share, "vocab", ring(zs, s))
        hidden = lax.dynamic_update_slice_in_dim(
            hidden, piece, lax.rem(zi - s + zs, zs) * share, 1
        )
    final = rms_norm(hidden.astype(F32), final_gain, 1e-05).astype(BF)
    logits = dot(final, all_head)
    vocab_rows = head_w.shape[0]
    local_ids = targets.reshape(rows) - zi * vocab_rows
    entry_ids = lax.broadcasted_iota(jnp.int32, (rows, vocab_rows), 1)
    picked = jnp.sum(jnp.where(entry_ids == local_ids[:, None], logits, 0.0), axis=-1)
    top = jnp.max(logits, axis=-1)
    exps = jnp.sum(jnp.exp(logits - top[:, None]), axis=-1)
    stats = jnp.stack([top, exps, picked])
    stats = lax.all_to_all(
        jnp.broadcast_to(stats[None], (zs, *stats.shape)), "vocab", 0, 0, tiled=True
    )
    all_top = jnp.max(stats[:, 0], axis=0)
    all_exps = jnp.sum(stats[:, 1] * jnp.exp(stats[:, 0] - all_top), axis=0)
    token_logp = (jnp.sum(stats[:, 2], axis=0) - (all_top + jnp.log(all_exps))).reshape(
        batch_count, local_len
    )
    positions = lax.axis_index(DP) * local_len + jnp.arange(local_len, dtype=jnp.int32)
    valid = positions[None, :] < lengths[:, None]
    masked = jnp.sum(jnp.where(valid, token_logp, 0.0))
    peers = YS * XS * CS
    sums = lax.all_to_all(jnp.broadcast_to(masked, (peers, 1)), DP, 0, 0, tiled=True)
    mean_logp = jnp.sum(sums) / jnp.sum(lengths.astype(F32))
    return (hidden_share.reshape(batch_count, local_len, share), token_logp, mean_logp)


def solution(mesh):
    split = Mesh(mesh.devices.reshape(YS, XS, CS, mesh.shape["vocab"]), (*DP, "vocab"))
    return jax.shard_map(
        body,
        mesh=split,
        in_specs=(
            P(None, DP, None),
            P(),
            P(DP, "vocab"),
            P(DP, "vocab"),
            P(None, "vocab"),
            P("vocab"),
            P("vocab", None),
            P("vocab", None),
            P(),
            P(None, "vocab"),
            P("vocab"),
            P("vocab", None),
            P("vocab", None),
            P(),
            P("vocab", DP),
            P(None, DP),
            P(),
        ),
        out_specs=(P(None, DP, "vocab"), P(None, DP), P()),
        check_vma=False,
    )
```

```python
import math

import jax
import jax.numpy as jnp
from jax import lax
from jax.experimental import pallas as pl
from jax.experimental.pallas import tpu as pltpu
from jax.sharding import Mesh
from jax.sharding import PartitionSpec as P

DP = ("dp_0", "dp_1", "dp_2")
CHIPS = ("dp_0", "dp_1")
YS, XS, CS = 4, 4, 2
BF = jnp.bfloat16
F32 = jnp.float32
LOG2E = math.log2(math.e)


def place(y, x, c):
    return ((y % YS) * XS + x % XS) * CS + c


def turns(by, phase):
    pairs = []
    for y in range(YS):
        for x in range(XS):
            for c in range(CS):
                along_x = (c == 0) == (phase == 0)
                to = place(y, x + by, c) if along_x else place(y + by, x, c)
                pairs.append((place(y, x, c), to))
    return pairs


def ring(peers, by):
    return [(i, (i + by) % peers) for i in range(peers)]


def swap_cores(array):
    return lax.ppermute(array, "dp_2", ring(CS, 1))


def around(array, axis, hops):
    middle = array.shape[0] // 2
    behind = lax.ppermute(array, axis, hops(1))
    ahead = lax.ppermute(array, axis, hops(3))
    first = lax.ppermute(behind[:middle], axis, hops(1))
    second = lax.ppermute(ahead[middle:], axis, hops(3))
    return behind, (first, second), ahead


def blocks_in_order(y, x, core):
    found = []
    for s2 in range(4):
        for s1 in range(4):
            first = lax.rem(y - s2 + YS, YS) * XS + lax.rem(x - s1 + XS, XS)
            second = lax.rem(y - s1 + YS, YS) * XS + lax.rem(x - s2 + XS, XS)
            found.append(jnp.where(core == 0, first, second) * CS + core)
    return found


def rms_norm(values, gain, epsilon):
    return values * lax.rsqrt(jnp.mean(values * values, axis=-1, keepdims=True) + epsilon) * gain


def dot(a, b):
    return jnp.dot(a, b, preferred_element_type=F32)


def norm_kernel(wide, order, resid, tail, gain, normed, mine, theirs, tail_normed):
    rows, halo = resid.shape[0], tail.shape[0]
    for r in range(0, rows, 32):
        normed[r : r + 32] = rms_norm(resid[r : r + 32].astype(F32), gain[...], 1e-05).astype(BF)
    tail_normed[...] = rms_norm(tail[...].astype(F32), gain[...], 1e-05).astype(BF)
    count = mine.shape[1] // wide
    for k in range(2 * count):
        out = (mine, theirs)[k // count]
        at = pl.ds(pl.multiple_of(order[k] * wide, wide), wide)
        to = slice((k % count) * wide, (k % count + 1) * wide)
        out[:rows, to] = normed[:, at]
        out[rows : rows + halo, to] = tail_normed[:, at]


def steps_kernel(rows, length, nstate, bc, dt, gain, proj, bias, conv, rate, step3, du3, last, total):
    raw = dt[...]
    normed = rms_norm(raw, gain[...], 1e-06).astype(BF)
    v = dot(normed, proj[...]) + bias[...]
    step = jnp.maximum(v, 0.0) + jnp.log1p(jnp.exp(-jnp.abs(v)))
    du = step * conv[...]
    for j in range(step3.shape[1]):
        step3[:, j, :] = step[:, j * 128 : (j + 1) * 128]
        du3[:, j, :] = du[:, j * 128 : (j + 1) * 128]
    batches = rows // length

    def advance(t, carry):
        state, sums = carry
        state, sums = list(state), list(sums)
        for b in range(batches):
            at = b * length + t
            s, u = step3[at], du3[at]
            sums[b] = sums[b] + s
            for n in range(nstate):
                k = b * nstate + n
                state[k] = jnp.exp2(s * rate[n]) * state[k] + u * bc[at * 2 * nstate + n]
        return tuple(state), tuple(sums)

    zero = jnp.zeros(step3.shape[1:], F32)
    state, sums = lax.fori_loop(
        0, length, advance, ((zero,) * (batches * nstate), (zero,) * batches), unroll=2
    )
    for b in range(batches):
        total[b] = sums[b]
        for n in range(nstate):
            last[b, n] = state[b * nstate + n]


def outputs_kernel(rows, length, nstate, bc, step3, du3, rate, start, z, gated, y3):
    batches = rows // length

    def advance(t, state):
        state = list(state)
        for b in range(batches):
            at = b * length + t
            s, u = step3[at], du3[at]
            y = None
            for n in range(nstate):
                k = b * nstate + n
                state[k] = jnp.exp2(s * rate[n]) * state[k] + u * bc[at * 2 * nstate + n]
                part = state[k] * bc[at * 2 * nstate + nstate + n]
                y = part if y is None else y + part
            y3[at] = y
        return tuple(state)

    state = tuple(start[b, n] for b in range(batches) for n in range(nstate))
    lax.fori_loop(0, length, advance, state, unroll=2)
    for j in range(y3.shape[1]):
        gate = z[:, j * 128 : (j + 1) * 128].astype(F32)
        gate = gate / (1.0 + jnp.exp(-gate))
        gated[:, j * 128 : (j + 1) * 128] = (y3[:, j, :] * gate).astype(BF)


def scaled_dot(j, order, deep, lhs, gain, head):
    values = lhs.astype(F32)
    at = pl.ds(pl.multiple_of(order[j] * deep, deep), deep)
    squares = jnp.sum(values * values, axis=-1, keepdims=True)
    return dot((values * gain[:, at]).astype(BF), head[...]), squares


def add_blocks(pieces, order, gain, head, before, acc, squares):
    deep = head.shape[0]
    per = pieces[0].shape[1] // deep
    for j in range(len(pieces) // 2 * per):

        @pl.when(pl.program_id(0) == j)
        def _():
            cut = slice(j % per * deep, (j % per + 1) * deep)
            upper, lower = pieces[j // per * 2 : j // per * 2 + 2]
            lhs = jnp.concatenate([upper[:, cut], lower[:, cut]], axis=0)
            product, part = scaled_dot(j, order, deep, lhs, gain, head)
            part = jnp.broadcast_to(part, squares.shape)
            if j > 0:
                acc[...] += product
                squares[...] += part
            elif before:
                acc[...] = product + before[0][...]
                squares[...] = part + before[1][...]
            else:
                acc[...] = product
                squares[...] = part


def own_kernel(order, upper, lower, gain, head, acc, squares):
    add_blocks((upper, lower), order, gain, head, None, acc, squares)


def near_kernel(order, a, b, c, d, gain, head, acc_in, squares_in, acc, squares):
    add_blocks((a, b, c, d), order, gain, head, (acc_in, squares_in), acc, squares)


def last_kernel(order, upper, lower, gain, head, acc_in, squares_in, ids, stats, acc, squares):
    add_blocks((upper, lower), order, gain, head, (acc_in, squares_in), acc, squares)
    per = upper.shape[1] // head.shape[0]
    width = gain.shape[1]

    @pl.when(pl.program_id(0) == per - 1)
    def _():
        rows, some = acc.shape[0], 16
        lane = lax.broadcasted_iota(jnp.int32, (some, 128), 1)
        entry = lax.broadcasted_iota(jnp.int32, (some, acc.shape[1]), 1)
        for r in range(0, rows, some):
            cut = slice(r, r + some)
            logits = acc[cut] * lax.rsqrt(squares[cut, :1] / width + 1e-05)
            top = jnp.max(logits, axis=-1, keepdims=True)
            exps = jnp.sum(jnp.exp(logits - top), axis=-1, keepdims=True)
            picked = jnp.sum(jnp.where(entry == ids[cut], logits, 0.0), axis=-1, keepdims=True)
            stats[cut] = jnp.where(lane == 0, top, jnp.where(lane == 1, exps, picked))


def vmem():
    return pl.BlockSpec(memory_space=pltpu.VMEM)


def smem():
    return pl.BlockSpec(memory_space=pltpu.SMEM)


def body(
    resid,
    norm_gain,
    in_x,
    in_z,
    conv_w,
    conv_b,
    xdt_w,
    xbc_w,
    dt_gain,
    dt_proj,
    dt_bias,
    a_rate,
    out_w,
    final_gain,
    head_w,
    targets,
    lengths,
):
    batch_count, local_len, width = resid.shape
    k_rows, channels = in_x.shape
    nstate = a_rate.shape[1]
    taps = conv_w.shape[0]
    rank = xdt_w.shape[1]
    rows = batch_count * local_len
    y, x, core = (lax.axis_index(a) for a in DP)
    zi = lax.axis_index("vocab")
    zs = lax.axis_size("vocab")

    order = [(i, i + 1) for i in range(YS * XS * CS - 1)]
    tail = lax.ppermute(resid[:, local_len - (taps - 1) :, :], DP, order)
    near = {s: lax.ppermute(in_x, DP, turns(s, 0)) for s in (1, 3, 2)}
    line = jnp.concatenate([in_x, near[1], near[2], near[3]], axis=0)
    halo = 16
    tail = jnp.pad(
        tail.reshape(batch_count * (taps - 1), width),
        ((0, halo - batch_count * (taps - 1)), (0, 0)),
    )
    flat = resid.reshape(rows, width)
    half_rows = jax.ShapeDtypeStruct((rows + halo, width // CS), BF)
    normed, mine, theirs = pl.pallas_call(
        lambda *refs: norm_kernel(k_rows, *refs),
        out_shape=(jax.ShapeDtypeStruct((rows, width), BF), half_rows, half_rows),
        in_specs=[smem()] + [vmem()] * 3,
        out_specs=(vmem(),) * 3,
        scratch_shapes=[pltpu.VMEM((halo, width), BF)],
        compiler_params=pltpu.CompilerParams(vmem_limit_bytes=48 << 20),
        name="norm",
    )(
        jnp.stack(blocks_in_order(y, x, core) + blocks_in_order(y, x, 1 - core)),
        flat,
        tail,
        norm_gain.reshape(1, width),
    )
    line, mine, theirs, in_z = lax.optimization_barrier((line, mine, theirs, in_z))
    all_z = lax.all_gather(in_z, DP, axis=0, tiled=True)
    behind, opposite, ahead = around(line, DP, lambda by: turns(by, 1))
    share = width // zs
    out_cut = [
        lax.dynamic_slice_in_dim(out_w, lax.rem(zi + by, zs) * share, share, 1)
        for by in range(zs)
    ]
    opposite, out_cut = lax.optimization_barrier((opposite, out_cut))
    pieces = [line, behind, jnp.concatenate(opposite, axis=0), ahead]
    theirs = swap_cores(theirs)
    depth = width // CS // 4
    cut = [slice(s * depth, (s + 1) * depth) for s in range(4)]
    turn = (0, 1, 3, 2)
    for_them = sum(dot(theirs[:, cut[s]], pieces[s]) for s in turn)
    from_them = swap_cores(for_them.astype(BF))
    x_acc = sum(dot(mine[:, cut[s]], pieces[s]) for s in turn) + from_them.astype(F32)
    x_all = x_acc.astype(BF)
    x_inner = x_all[:rows].reshape(batch_count, local_len, channels)
    before = x_all[rows : rows + batch_count * (taps - 1)].reshape(batch_count, taps - 1, channels)
    padded = jnp.concatenate([before, x_inner], axis=1).astype(F32)
    conv_sum = jnp.zeros((batch_count, local_len, channels), F32) + conv_b
    for k in range(taps):
        conv_sum = conv_sum + conv_w[k] * padded[:, k : k + local_len, :]
    conv_act = jax.nn.silu(conv_sum).reshape(rows, channels)
    low = dot(conv_act.astype(BF), jnp.concatenate([xdt_w, xbc_w], axis=1))
    low_sent = low.astype(BF)
    low_sum = low_sent.astype(F32)
    for s in (1, 3, 2):
        low_sum = low_sum + lax.ppermute(low_sent, "vocab", ring(zs, s)).astype(F32)
    head_t, _, _ = lax.optimization_barrier((head_w.T, all_z, low_sum))
    all_head = lax.all_gather(head_t, DP, axis=0, tiled=True)
    dt_raw = low_sum[:, :rank]
    bc_raw = low_sum[:, rank:].reshape(-1)

    fold = channels // 128
    rate = (a_rate.T * (-LOG2E)).reshape(nstate, fold, 128)
    seq = jax.ShapeDtypeStruct((rows, fold, 128), F32)
    step3, du3, last, total = pl.pallas_call(
        lambda *refs: steps_kernel(rows, local_len, nstate, *refs),
        out_shape=(
            seq,
            seq,
            jax.ShapeDtypeStruct((batch_count, nstate, fold, 128), F32),
            jax.ShapeDtypeStruct((batch_count, fold, 128), F32),
        ),
        in_specs=[smem()] + [vmem()] * 6,
        out_specs=(vmem(),) * 4,
        compiler_params=pltpu.CompilerParams(vmem_limit_bytes=48 << 20),
        name="steps",
    )(
        bc_raw,
        dt_raw,
        dt_gain.reshape(1, rank),
        dt_proj,
        dt_bias.reshape(1, channels),
        conv_act,
        rate,
    )

    half = nstate // CS
    own = lax.dynamic_slice_in_dim(last, core * half, half, 1)
    other = lax.dynamic_slice_in_dim(last, (1 - core) * half, half, 1)
    rate_half = lax.dynamic_slice_in_dim(rate, core * half, half, 0)
    sent = jnp.concatenate([other, total[:, None]], axis=1)
    got = swap_cores(sent)
    state_0 = jnp.where(core == 0, own, got[:, :half])
    state_1 = jnp.where(core == 0, got[:, :half], own)
    total_0 = jnp.where(core == 0, total, got[:, half])
    total_1 = jnp.where(core == 0, got[:, half], total)

    def decay(steps):
        return jnp.exp2(steps[:, None] * rate_half)

    chip_state = decay(total_1) * state_0 + state_1
    chip_total = total_0 + total_1
    coarse = chip_total.astype(BF)
    fine = (chip_total - coarse.astype(F32)).astype(BF)
    packed = jnp.concatenate(
        [chip_state.astype(BF), coarse[:, None], fine[:, None]], axis=1
    )
    chips = YS * XS
    everyone = lax.all_to_all(
        jnp.broadcast_to(packed[None], (chips, *packed.shape)), CHIPS, 0, 0, tiled=True
    )
    z_gate = dot(normed, all_z).astype(BF)
    everyone, z_gate = lax.optimization_barrier((everyone, z_gate))
    chip = y * XS + x
    enter = jnp.zeros_like(chip_state)
    for k in range(chips - 1):
        part = everyone[k].astype(F32)
        later = decay(part[:, half] + part[:, half + 1]) * enter + part[:, :half]
        enter = jnp.where(k < chip, later, enter)
    enter_1 = decay(total_0) * enter + state_0
    kept = jnp.where(core == 0, enter, enter_1)
    given = swap_cores(jnp.where(core == 0, enter_1, enter))
    start = jnp.concatenate(
        [jnp.where(core == 0, kept, given), jnp.where(core == 0, given, kept)], axis=1
    )

    gated = pl.pallas_call(
        lambda *refs: outputs_kernel(rows, local_len, nstate, *refs),
        out_shape=jax.ShapeDtypeStruct((rows, channels), BF),
        in_specs=[smem()] + [vmem()] * 5,
        out_specs=vmem(),
        scratch_shapes=[pltpu.VMEM((rows, fold, 128), F32)],
        compiler_params=pltpu.CompilerParams(vmem_limit_bytes=48 << 20),
        name="outputs",
    )(bc_raw, step3, du3, rate, start, z_gate)

    def hops(by):
        return ring(zs, by)

    middle = rows // 2
    far = dot(gated, out_cut[2]).astype(BF)
    up = lax.ppermute(far[:middle], "vocab", hops(1))
    down = lax.ppermute(far[middle:], "vocab", hops(3))
    after = dot(gated, out_cut[1])
    prior = dot(gated, out_cut[3])
    part = lax.dynamic_slice_in_dim(flat, zi * share, share, 1).astype(F32)
    mixer = dot(gated, out_cut[0]) + part
    up, mixer = lax.optimization_barrier((up, mixer))
    up_low = lax.ppermute(after[middle:].astype(BF), "vocab", hops(1))
    down_high = lax.ppermute(prior[:middle].astype(BF), "vocab", hops(3))
    up_high = lax.ppermute(
        (after[:middle] + up.astype(F32)).astype(BF), "vocab", hops(1)
    )
    down_low = lax.ppermute(
        (prior[middle:] + down.astype(F32)).astype(BF), "vocab", hops(3)
    )
    upper = (mixer[:middle] + (up_high.astype(F32) + down_high.astype(F32))).astype(BF)
    lower = (mixer[middle:] + (up_low.astype(F32) + down_low.astype(F32))).astype(BF)
    hidden_share = jnp.concatenate([upper, lower], axis=0)

    behind_upper = lax.ppermute(upper, "vocab", hops(1))
    ahead_lower = lax.ppermute(lower, "vocab", hops(3))
    behind_lower = lax.ppermute(lower, "vocab", hops(1))
    ahead_upper = lax.ppermute(upper, "vocab", hops(3))
    opposite_upper = lax.ppermute(behind_upper, "vocab", hops(1))
    opposite_lower = lax.ppermute(ahead_lower, "vocab", hops(3))
    vocab_rows = head_w.shape[0]
    deep = 512
    per = share // deep
    gain = final_gain.reshape(1, width)

    def blocks(*hops_back):
        firsts = [lax.rem(zi - s + zs, zs) * per for s in hops_back]
        return jnp.stack([first + i for first in firsts for i in range(per)])

    def whole(*shape):
        return pl.BlockSpec(shape, lambda j, order: (0,) * len(shape))

    head_block = pl.BlockSpec((deep, vocab_rows), lambda j, order: (order[j], 0))
    sums = [whole(rows, vocab_rows), whole(rows, 128)]
    sums_shape = (
        jax.ShapeDtypeStruct((rows, vocab_rows), F32),
        jax.ShapeDtypeStruct((rows, 128), F32),
    )

    def logits_call(kernel, name, from_where, pieces, extra, last=False):
        halves = [whole(middle, share)] * len(pieces)
        weights = [whole(1, width), head_block]
        extra_specs = [whole(*e.shape) for e in extra]
        return pl.pallas_call(
            kernel,
            grid_spec=pltpu.PrefetchScalarGridSpec(
                num_scalar_prefetch=1,
                grid=(len(pieces) // 2 * per,),
                in_specs=halves + weights + extra_specs,
                out_specs=whole(rows, 128) if last else tuple(sums),
                scratch_shapes=[pltpu.VMEM(s.shape, F32) for s in sums_shape] if last else [],
            ),
            out_shape=jax.ShapeDtypeStruct((rows, 128), F32) if last else sums_shape,
            compiler_params=pltpu.CompilerParams(vmem_limit_bytes=48 << 20),
            name=name,
        )(blocks(*from_where), *pieces, gain, all_head, *extra)

    acc = logits_call(own_kernel, "own_logits", (0,), (upper, lower), ())
    acc = logits_call(
        near_kernel,
        "near_logits",
        (1, 3),
        (behind_upper, behind_lower, ahead_upper, ahead_lower),
        acc,
    )
    local_ids = targets.reshape(rows, 1) - zi * vocab_rows
    stats = logits_call(
        last_kernel,
        "last_logits",
        (2,),
        (opposite_upper, opposite_lower),
        (*acc, local_ids),
        True,
    )
    stats = stats[:, :3].T
    stats = lax.all_to_all(
        jnp.broadcast_to(stats[None], (zs, *stats.shape)), "vocab", 0, 0, tiled=True
    )
    all_top = jnp.max(stats[:, 0], axis=0)
    all_exps = jnp.sum(stats[:, 1] * jnp.exp(stats[:, 0] - all_top), axis=0)
    token_logp = (jnp.sum(stats[:, 2], axis=0) - (all_top + jnp.log(all_exps))).reshape(
        batch_count, local_len
    )
    positions = lax.axis_index(DP) * local_len + jnp.arange(local_len, dtype=jnp.int32)
    valid = positions[None, :] < lengths[:, None]
    masked = jnp.sum(jnp.where(valid, token_logp, 0.0))
    peers = YS * XS * CS
    sums = lax.all_to_all(jnp.broadcast_to(masked, (peers, 1)), DP, 0, 0, tiled=True)
    mean_logp = jnp.sum(sums) / jnp.sum(lengths.astype(F32))
    return (hidden_share.reshape(batch_count, local_len, share), token_logp, mean_logp)


def solution(mesh):
    split = Mesh(mesh.devices.reshape(YS, XS, CS, mesh.shape["vocab"]), (*DP, "vocab"))
    return jax.shard_map(
        body,
        mesh=split,
        in_specs=(
            P(None, DP, None),
            P(),
            P(DP, "vocab"),
            P(DP, "vocab"),
            P(None, "vocab"),
            P("vocab"),
            P("vocab", None),
            P("vocab", None),
            P(),
            P(None, "vocab"),
            P("vocab"),
            P("vocab", None),
            P("vocab", None),
            P(),
            P("vocab", DP),
            P(None, DP),
            P(),
        ),
        out_specs=(P(None, DP, "vocab"), P(None, DP), P()),
        check_vma=False,
    )
```

```python
import math

import jax
import jax.numpy as jnp
from jax import lax
from jax.experimental import pallas as pl
from jax.experimental.pallas import tpu as pltpu
from jax.sharding import Mesh
from jax.sharding import PartitionSpec as P

DP = ("dp_0", "dp_1", "dp_2")
CHIPS = ("dp_0", "dp_1")
YS, XS, CS = 4, 4, 2
BF = jnp.bfloat16
F32 = jnp.float32
LOG2E = math.log2(math.e)


def place(y, x, c):
    return ((y % YS) * XS + x % XS) * CS + c


def turns(by, phase):
    pairs = []
    for y in range(YS):
        for x in range(XS):
            for c in range(CS):
                along_x = (c == 0) == (phase == 0)
                to = place(y, x + by, c) if along_x else place(y + by, x, c)
                pairs.append((place(y, x, c), to))
    return pairs


def ring(peers, by):
    return [(i, (i + by) % peers) for i in range(peers)]


def swap_cores(array):
    return lax.ppermute(array, "dp_2", ring(CS, 1))


def blocks_in_order(y, x, core):
    found = []
    for s2 in range(4):
        for s1 in range(4):
            first = lax.rem(y - s2 + YS, YS) * XS + lax.rem(x - s1 + XS, XS)
            second = lax.rem(y - s1 + YS, YS) * XS + lax.rem(x - s2 + XS, XS)
            found.append(jnp.where(core == 0, first, second) * CS + core)
    return found


def rms_norm(values, gain, epsilon):
    return values * lax.rsqrt(jnp.mean(values * values, axis=-1, keepdims=True) + epsilon) * gain


def dot(a, b):
    return jnp.dot(a, b, preferred_element_type=F32)


def norm_kernel(wide, order, resid, tail, gain, normed, mine, theirs, tail_normed):
    rows, halo = resid.shape[0], tail.shape[0]
    for r in range(0, rows, 32):
        normed[r : r + 32] = rms_norm(resid[r : r + 32].astype(F32), gain[...], 1e-05).astype(BF)
    tail_normed[...] = rms_norm(tail[...].astype(F32), gain[...], 1e-05).astype(BF)
    count = mine.shape[1] // wide
    for k in range(2 * count):
        out = (mine, theirs)[k // count]
        at = pl.ds(pl.multiple_of(order[k] * wide, wide), wide)
        to = slice((k % count) * wide, (k % count + 1) * wide)
        out[:rows, to] = normed[:, at]
        out[rows : rows + halo, to] = tail_normed[:, at]


def steps_kernel(rows, length, nstate, bc, dt, gain, proj, bias, conv, rate, step3, du3, last, total):
    raw = dt[...]
    normed = rms_norm(raw, gain[...], 1e-06).astype(BF)
    v = dot(normed, proj[...]) + bias[...]
    step = jnp.maximum(v, 0.0) + jnp.log1p(jnp.exp(-jnp.abs(v)))
    du = step * conv[...]
    for j in range(step3.shape[1]):
        step3[:, j, :] = step[:, j * 128 : (j + 1) * 128]
        du3[:, j, :] = du[:, j * 128 : (j + 1) * 128]
    batches = rows // length

    def advance(t, carry):
        state, sums = carry
        state, sums = list(state), list(sums)
        for b in range(batches):
            at = b * length + t
            s, u = step3[at], du3[at]
            sums[b] = sums[b] + s
            for n in range(nstate):
                k = b * nstate + n
                state[k] = jnp.exp2(s * rate[n]) * state[k] + u * bc[at * 2 * nstate + n]
        return tuple(state), tuple(sums)

    zero = jnp.zeros(step3.shape[1:], F32)
    state, sums = lax.fori_loop(
        0, length, advance, ((zero,) * (batches * nstate), (zero,) * batches), unroll=4
    )
    for b in range(batches):
        total[b] = sums[b]
        for n in range(nstate):
            last[b, n] = state[b * nstate + n]


def outputs_kernel(rows, length, nstate, bc, step3, du3, rate, start, z, gated, y3):
    batches = rows // length

    def advance(t, state):
        state = list(state)
        for b in range(batches):
            at = b * length + t
            s, u = step3[at], du3[at]
            y = None
            for n in range(nstate):
                k = b * nstate + n
                state[k] = jnp.exp2(s * rate[n]) * state[k] + u * bc[at * 2 * nstate + n]
                part = state[k] * bc[at * 2 * nstate + nstate + n]
                y = part if y is None else y + part
            y3[at] = y
        return tuple(state)

    state = tuple(start[b, n] for b in range(batches) for n in range(nstate))
    lax.fori_loop(0, length, advance, state, unroll=4)
    for j in range(y3.shape[1]):
        gate = z[:, j * 128 : (j + 1) * 128].astype(F32)
        gate = gate / (1.0 + jnp.exp(-gate))
        gated[:, j * 128 : (j + 1) * 128] = (y3[:, j, :] * gate).astype(BF)


def scaled_dot(j, order, deep, lhs, gain, head):
    values = lhs.astype(F32)
    at = pl.ds(pl.multiple_of(order[j] * deep, deep), deep)
    squares = jnp.sum(values * values, axis=-1, keepdims=True)
    return dot((values * gain[:, at]).astype(BF), head[...]), squares


def add_blocks(pieces, order, gain, head, before, acc, squares):
    deep = head.shape[0]
    per = pieces[0].shape[1] // deep
    for j in range(len(pieces) // 2 * per):

        @pl.when(pl.program_id(0) == j)
        def _():
            cut = slice(j % per * deep, (j % per + 1) * deep)
            upper, lower = pieces[j // per * 2 : j // per * 2 + 2]
            lhs = jnp.concatenate([upper[:, cut], lower[:, cut]], axis=0)
            product, part = scaled_dot(j, order, deep, lhs, gain, head)
            part = jnp.broadcast_to(part, squares.shape)
            if j > 0:
                acc[...] += product
                squares[...] += part
            elif before:
                acc[...] = product + before[0][...]
                squares[...] = part + before[1][...]
            else:
                acc[...] = product
                squares[...] = part


def near_kernel(order, a, b, c, d, e, f, gain, head, acc, squares):
    add_blocks((a, b, c, d, e, f), order, gain, head, None, acc, squares)


def last_kernel(order, upper, lower, gain, head, acc_in, squares_in, ids, stats, acc, squares):
    add_blocks((upper, lower), order, gain, head, (acc_in, squares_in), acc, squares)
    per = upper.shape[1] // head.shape[0]
    width = gain.shape[1]

    @pl.when(pl.program_id(0) == per - 1)
    def _():
        rows, some = acc.shape[0], 16
        lane = lax.broadcasted_iota(jnp.int32, (some, 128), 1)
        entry = lax.broadcasted_iota(jnp.int32, (some, acc.shape[1]), 1)
        for r in range(0, rows, some):
            cut = slice(r, r + some)
            logits = acc[cut] * lax.rsqrt(squares[cut, :1] / width + 1e-05)
            top = jnp.max(logits, axis=-1, keepdims=True)
            exps = jnp.sum(jnp.exp(logits - top), axis=-1, keepdims=True)
            picked = jnp.sum(jnp.where(entry == ids[cut], logits, 0.0), axis=-1, keepdims=True)
            stats[cut] = jnp.where(lane == 0, top, jnp.where(lane == 1, exps, picked))


def pieces_kernel(lhs, *refs):
    at, total = 0, None
    for w in refs[:-1]:
        deep = w.shape[0]
        part = dot(lhs[:, at : at + deep], w[...])
        total = part if total is None else total + part
        at += deep
    refs[-1][...] = total.astype(refs[-1].dtype)


def finish_kernel(base, lengths, stats, token, sums):
    tops = [stats[k, 0:1] for k in range(stats.shape[0])]
    top = tops[0]
    for t in tops[1:]:
        top = jnp.maximum(top, t)
    exps = sum(stats[k, 1:2] * jnp.exp(t - top) for k, t in enumerate(tops))
    picked = sum(stats[k, 2:3] for k in range(stats.shape[0]))
    logp = picked - (top + jnp.log(exps))
    batches, length = token.shape
    position = base[0] + lax.broadcasted_iota(jnp.int32, (1, length), 1)
    total = jnp.zeros((1, 1), F32)
    for b in range(batches):
        part = logp[:, b * length : (b + 1) * length]
        token[b : b + 1] = part
        masked = jnp.where(position < lengths[b], part, 0.0)
        total = total + jnp.sum(masked, axis=1, keepdims=True)
    sums[...] = jnp.broadcast_to(total[None], sums.shape)


def vmem():
    return pl.BlockSpec(memory_space=pltpu.VMEM)


def smem():
    return pl.BlockSpec(memory_space=pltpu.SMEM)


def body(
    resid,
    norm_gain,
    in_x,
    in_z,
    conv_w,
    conv_b,
    xdt_w,
    xbc_w,
    dt_gain,
    dt_proj,
    dt_bias,
    a_rate,
    out_w,
    final_gain,
    head_w,
    targets,
    lengths,
):
    batch_count, local_len, width = resid.shape
    k_rows, channels = in_x.shape
    nstate = a_rate.shape[1]
    taps = conv_w.shape[0]
    rank = xdt_w.shape[1]
    rows = batch_count * local_len
    y, x, core = (lax.axis_index(a) for a in DP)
    zi = lax.axis_index("vocab")
    zs = lax.axis_size("vocab")

    order = [(i, i + 1) for i in range(YS * XS * CS - 1)]
    tail = lax.ppermute(resid[:, local_len - (taps - 1) :, :], DP, order)
    near = {s: lax.ppermute(in_x, DP, turns(s, 0)) for s in (1, 3, 2)}
    first = jnp.concatenate([in_x, near[1]], axis=0)
    second = jnp.concatenate([near[2], near[3]], axis=0)
    halo = 16
    tail = jnp.pad(
        tail.reshape(batch_count * (taps - 1), width),
        ((0, halo - batch_count * (taps - 1)), (0, 0)),
    )
    flat = resid.reshape(rows, width)
    half_rows = jax.ShapeDtypeStruct((rows + halo, width // CS), BF)
    normed, mine, theirs = pl.pallas_call(
        lambda *refs: norm_kernel(k_rows, *refs),
        out_shape=(jax.ShapeDtypeStruct((rows, width), BF), half_rows, half_rows),
        in_specs=[smem()] + [vmem()] * 3,
        out_specs=(vmem(),) * 3,
        scratch_shapes=[pltpu.VMEM((halo, width), BF)],
        compiler_params=pltpu.CompilerParams(vmem_limit_bytes=48 << 20),
        name="norm",
    )(
        jnp.stack(blocks_in_order(y, x, core) + blocks_in_order(y, x, 1 - core)),
        flat,
        tail,
        norm_gain.reshape(1, width),
    )
    first, second, mine, theirs, in_z = lax.optimization_barrier(
        (first, second, mine, theirs, in_z)
    )
    all_z = lax.all_gather(in_z, DP, axis=0, tiled=True)
    behind_first = lax.ppermute(first, DP, turns(1, 1))
    ahead_second = lax.ppermute(second, DP, turns(3, 1))
    behind_second = lax.ppermute(second, DP, turns(1, 1))
    ahead_first = lax.ppermute(first, DP, turns(3, 1))
    far_first = lax.ppermute(behind_first, DP, turns(1, 1))
    far_second = lax.ppermute(ahead_second, DP, turns(3, 1))
    share = width // zs
    out_cut = [
        lax.dynamic_slice_in_dim(out_w, lax.rem(zi + by, zs) * share, share, 1)
        for by in range(zs)
    ]
    far_first, far_second, out_cut = lax.optimization_barrier((far_first, far_second, out_cut))
    pieces = [
        first, second, behind_first, behind_second, far_first, far_second, ahead_first, ahead_second
    ]

    def half_dot(lhs, kind, name):
        return pl.pallas_call(
            pieces_kernel,
            out_shape=jax.ShapeDtypeStruct((lhs.shape[0], channels), kind),
            in_specs=[vmem()] * (1 + len(pieces)),
            out_specs=vmem(),
            compiler_params=pltpu.CompilerParams(vmem_limit_bytes=48 << 20),
            name=name,
        )(lhs, *pieces)

    theirs = swap_cores(theirs)
    from_them = swap_cores(half_dot(theirs, BF, "x_theirs"))
    x_acc = half_dot(mine, F32, "x_mine") + from_them.astype(F32)
    x_all = x_acc.astype(BF)
    x_inner = x_all[:rows].reshape(batch_count, local_len, channels)
    before = x_all[rows : rows + batch_count * (taps - 1)].reshape(batch_count, taps - 1, channels)
    padded = jnp.concatenate([before, x_inner], axis=1).astype(F32)
    conv_sum = jnp.zeros((batch_count, local_len, channels), F32) + conv_b
    for k in range(taps):
        conv_sum = conv_sum + conv_w[k] * padded[:, k : k + local_len, :]
    conv_act = jax.nn.silu(conv_sum).reshape(rows, channels)
    low = dot(conv_act.astype(BF), jnp.concatenate([xdt_w, xbc_w], axis=1))
    low_sent = low.astype(BF)
    low_sum = low_sent.astype(F32)
    for s in (1, 3, 2):
        low_sum = low_sum + lax.ppermute(low_sent, "vocab", ring(zs, s)).astype(F32)
    head_t, _, _ = lax.optimization_barrier((head_w.T, all_z, low_sum))
    all_head = lax.all_gather(head_t, DP, axis=0, tiled=True)
    dt_raw = low_sum[:, :rank]
    bc_raw = low_sum[:, rank:].reshape(-1)

    fold = channels // 128
    rate = (a_rate.T * (-LOG2E)).reshape(nstate, fold, 128)
    seq = jax.ShapeDtypeStruct((rows, fold, 128), F32)
    step3, du3, last, total = pl.pallas_call(
        lambda *refs: steps_kernel(rows, local_len, nstate, *refs),
        out_shape=(
            seq,
            seq,
            jax.ShapeDtypeStruct((batch_count, nstate, fold, 128), F32),
            jax.ShapeDtypeStruct((batch_count, fold, 128), F32),
        ),
        in_specs=[smem()] + [vmem()] * 6,
        out_specs=(vmem(),) * 4,
        compiler_params=pltpu.CompilerParams(vmem_limit_bytes=48 << 20),
        name="steps",
    )(
        bc_raw,
        dt_raw,
        dt_gain.reshape(1, rank),
        dt_proj,
        dt_bias.reshape(1, channels),
        conv_act,
        rate,
    )

    half = nstate // CS
    own = lax.dynamic_slice_in_dim(last, core * half, half, 1)
    other = lax.dynamic_slice_in_dim(last, (1 - core) * half, half, 1)
    rate_half = lax.dynamic_slice_in_dim(rate, core * half, half, 0)
    sent = jnp.concatenate([other, total[:, None]], axis=1)
    got = swap_cores(sent)
    state_0 = jnp.where(core == 0, own, got[:, :half])
    state_1 = jnp.where(core == 0, got[:, :half], own)
    total_0 = jnp.where(core == 0, total, got[:, half])
    total_1 = jnp.where(core == 0, got[:, half], total)

    def decay(steps):
        return jnp.exp2(steps[:, None] * rate_half)

    chip_state = decay(total_1) * state_0 + state_1
    chip_total = total_0 + total_1
    coarse = chip_total.astype(BF)
    fine = (chip_total - coarse.astype(F32)).astype(BF)
    packed = jnp.concatenate(
        [chip_state.astype(BF), coarse[:, None], fine[:, None]], axis=1
    )
    chips = YS * XS
    everyone = lax.all_to_all(
        jnp.broadcast_to(packed[None], (chips, *packed.shape)), CHIPS, 0, 0, tiled=True
    )
    z_gate = dot(normed, all_z).astype(BF)
    everyone, z_gate = lax.optimization_barrier((everyone, z_gate))
    chip = y * XS + x
    enter = jnp.zeros_like(chip_state)
    for k in range(chips - 1):
        part = everyone[k].astype(F32)
        later = decay(part[:, half] + part[:, half + 1]) * enter + part[:, :half]
        enter = jnp.where(k < chip, later, enter)
    enter_1 = decay(total_0) * enter + state_0
    kept = jnp.where(core == 0, enter, enter_1)
    given = swap_cores(jnp.where(core == 0, enter_1, enter))
    start = jnp.concatenate(
        [jnp.where(core == 0, kept, given), jnp.where(core == 0, given, kept)], axis=1
    )

    gated = pl.pallas_call(
        lambda *refs: outputs_kernel(rows, local_len, nstate, *refs),
        out_shape=jax.ShapeDtypeStruct((rows, channels), BF),
        in_specs=[smem()] + [vmem()] * 5,
        out_specs=vmem(),
        scratch_shapes=[pltpu.VMEM((rows, fold, 128), F32)],
        compiler_params=pltpu.CompilerParams(vmem_limit_bytes=48 << 20),
        name="outputs",
    )(bc_raw, step3, du3, rate, start, z_gate)

    def hops(by):
        return ring(zs, by)

    middle = rows // 2
    far = dot(gated, out_cut[2]).astype(BF)
    up = lax.ppermute(far[:middle], "vocab", hops(1))
    down = lax.ppermute(far[middle:], "vocab", hops(3))
    after = dot(gated, out_cut[1])
    prior = dot(gated, out_cut[3])
    part = lax.dynamic_slice_in_dim(flat, zi * share, share, 1).astype(F32)
    mixer = dot(gated, out_cut[0]) + part
    up, mixer = lax.optimization_barrier((up, mixer))
    up_low = lax.ppermute(after[middle:].astype(BF), "vocab", hops(1))
    down_high = lax.ppermute(prior[:middle].astype(BF), "vocab", hops(3))
    up_high = lax.ppermute(
        (after[:middle] + up.astype(F32)).astype(BF), "vocab", hops(1)
    )
    down_low = lax.ppermute(
        (prior[middle:] + down.astype(F32)).astype(BF), "vocab", hops(3)
    )
    upper = (mixer[:middle] + (up_high.astype(F32) + down_high.astype(F32))).astype(BF)
    lower = (mixer[middle:] + (up_low.astype(F32) + down_low.astype(F32))).astype(BF)
    hidden_share = jnp.concatenate([upper, lower], axis=0)

    behind_upper = lax.ppermute(upper, "vocab", hops(1))
    ahead_lower = lax.ppermute(lower, "vocab", hops(3))
    behind_lower = lax.ppermute(lower, "vocab", hops(1))
    ahead_upper = lax.ppermute(upper, "vocab", hops(3))
    opposite_upper = lax.ppermute(behind_upper, "vocab", hops(1))
    opposite_lower = lax.ppermute(ahead_lower, "vocab", hops(3))
    vocab_rows = head_w.shape[0]
    gain = final_gain.reshape(1, width)

    def blocks(per, *hops_back):
        firsts = [lax.rem(zi - s + zs, zs) * per for s in hops_back]
        return jnp.stack([first + i for first in firsts for i in range(per)])

    def whole(*shape):
        return vmem()

    sums = [whole(rows, vocab_rows), whole(rows, 128)]
    sums_shape = (
        jax.ShapeDtypeStruct((rows, vocab_rows), F32),
        jax.ShapeDtypeStruct((rows, 128), F32),
    )

    def logits_call(kernel, name, deep, from_where, pieces, extra, last=False):
        per = share // deep
        head_block = pl.BlockSpec((deep, vocab_rows), lambda j, order: (order[j], 0))
        halves = [whole(middle, share)] * len(pieces)
        weights = [whole(1, width), head_block]
        extra_specs = [whole(*e.shape) for e in extra]
        return pl.pallas_call(
            kernel,
            grid_spec=pltpu.PrefetchScalarGridSpec(
                num_scalar_prefetch=1,
                grid=(len(pieces) // 2 * per,),
                in_specs=halves + weights + extra_specs,
                out_specs=whole(rows, 128) if last else tuple(sums),
                scratch_shapes=[pltpu.VMEM(s.shape, F32) for s in sums_shape] if last else [],
            ),
            out_shape=jax.ShapeDtypeStruct((rows, 128), F32) if last else sums_shape,
            compiler_params=pltpu.CompilerParams(vmem_limit_bytes=48 << 20),
            name=name,
        )(blocks(per, *from_where), *pieces, gain, all_head, *extra)

    acc = logits_call(
        near_kernel,
        "near_logits",
        share,
        (0, 1, 3),
        (upper, lower, behind_upper, behind_lower, ahead_upper, ahead_lower),
        (),
    )
    local_ids = targets.reshape(rows, 1) - zi * vocab_rows
    stats = logits_call(
        last_kernel,
        "last_logits",
        share // 2,
        (2,),
        (opposite_upper, opposite_lower),
        (*acc, local_ids),
        True,
    )
    stats = stats[:, :3].T
    stats = lax.all_to_all(
        jnp.broadcast_to(stats[None], (zs, *stats.shape)), "vocab", 0, 0, tiled=True
    )
    peers = YS * XS * CS
    token_logp, sums = pl.pallas_call(
        finish_kernel,
        out_shape=(
            jax.ShapeDtypeStruct((batch_count, local_len), F32),
            jax.ShapeDtypeStruct((peers, 1, 128), F32),
        ),
        in_specs=[smem(), smem(), vmem()],
        out_specs=(vmem(),) * 2,
        name="finish",
    )((lax.axis_index(DP) * local_len).reshape(1), lengths, stats)
    sums = lax.all_to_all(sums, DP, 0, 0, tiled=True)[:, 0, 0]
    mean_logp = jnp.sum(sums) / jnp.sum(lengths.astype(F32))
    return (hidden_share.reshape(batch_count, local_len, share), token_logp, mean_logp)


def solution(mesh):
    split = Mesh(mesh.devices.reshape(YS, XS, CS, mesh.shape["vocab"]), (*DP, "vocab"))
    return jax.shard_map(
        body,
        mesh=split,
        in_specs=(
            P(None, DP, None),
            P(),
            P(DP, "vocab"),
            P(DP, "vocab"),
            P(None, "vocab"),
            P("vocab"),
            P("vocab", None),
            P("vocab", None),
            P(),
            P(None, "vocab"),
            P("vocab"),
            P("vocab", None),
            P("vocab", None),
            P(),
            P("vocab", DP),
            P(None, DP),
            P(),
        ),
        out_specs=(P(None, DP, "vocab"), P(None, DP), P()),
        check_vma=False,
    )
```

```python
import math

import jax
import jax.numpy as jnp
from jax import lax
from jax.experimental import pallas as pl
from jax.experimental.pallas import tpu as pltpu
from jax.sharding import Mesh
from jax.sharding import PartitionSpec as P

DP = ("dp_0", "dp_1", "dp_2")
CHIPS = ("dp_0", "dp_1")
YS, XS, CS = 4, 4, 2
BF = jnp.bfloat16
F32 = jnp.float32
LOG2E = math.log2(math.e)


def place(y, x, c):
    return ((y % YS) * XS + x % XS) * CS + c


def turns(by, phase):
    pairs = []
    for y in range(YS):
        for x in range(XS):
            for c in range(CS):
                along_x = (c == 0) == (phase == 0)
                to = place(y, x + by, c) if along_x else place(y + by, x, c)
                pairs.append((place(y, x, c), to))
    return pairs


def ring(peers, by):
    return [(i, (i + by) % peers) for i in range(peers)]


def swap_cores(array):
    return lax.ppermute(array, "dp_2", ring(CS, 1))


def blocks_in_order(y, x, core):
    found = []
    for s2 in range(4):
        for s1 in range(4):
            first = lax.rem(y - s2 + YS, YS) * XS + lax.rem(x - s1 + XS, XS)
            second = lax.rem(y - s1 + YS, YS) * XS + lax.rem(x - s2 + XS, XS)
            found.append(jnp.where(core == 0, first, second) * CS + core)
    return found


def rms_norm(values, gain, epsilon):
    return values * lax.rsqrt(jnp.mean(values * values, axis=-1, keepdims=True) + epsilon) * gain


def dot(a, b):
    return jnp.dot(a, b, preferred_element_type=F32)


def norm_kernel(wide, order, resid, tail, gain, normed, mine, theirs, tail_normed):
    rows, halo = resid.shape[0], tail.shape[0]
    for r in range(0, rows, 32):
        normed[r : r + 32] = rms_norm(resid[r : r + 32].astype(F32), gain[...], 1e-05).astype(BF)
    tail_normed[...] = rms_norm(tail[...].astype(F32), gain[...], 1e-05).astype(BF)
    count = mine.shape[1] // wide
    for k in range(2 * count):
        out = (mine, theirs)[k // count]
        at = pl.ds(pl.multiple_of(order[k] * wide, wide), wide)
        to = slice((k % count) * wide, (k % count + 1) * wide)
        out[:rows, to] = normed[:, at]
        out[rows : rows + halo, to] = tail_normed[:, at]


def steps_kernel(rows, length, nstate, bc, dt, gain, proj, bias, conv, rate, step3, du3, last, total):
    raw = dt[...]
    normed = rms_norm(raw, gain[...], 1e-06).astype(BF)
    v = dot(normed, proj[...]) + bias[...]
    step = jnp.maximum(v, 0.0) + jnp.log1p(jnp.exp(-jnp.abs(v)))
    du = step * conv[...]
    for j in range(step3.shape[1]):
        step3[:, j, :] = step[:, j * 128 : (j + 1) * 128]
        du3[:, j, :] = du[:, j * 128 : (j + 1) * 128]
    batches = rows // length

    def advance(t, carry):
        state, sums = carry
        state, sums = list(state), list(sums)
        for b in range(batches):
            at = b * length + t
            s, u = step3[at], du3[at]
            sums[b] = sums[b] + s
            for n in range(nstate):
                k = b * nstate + n
                state[k] = jnp.exp2(s * rate[n]) * state[k] + u * bc[at * 2 * nstate + n]
        return tuple(state), tuple(sums)

    zero = jnp.zeros(step3.shape[1:], F32)
    state, sums = lax.fori_loop(
        0, length, advance, ((zero,) * (batches * nstate), (zero,) * batches), unroll=4
    )
    for b in range(batches):
        total[b] = sums[b]
        for n in range(nstate):
            last[b, n] = state[b * nstate + n]


def outputs_kernel(rows, length, nstate, bc, step3, du3, rate, start, z, gated, y3):
    batches = rows // length

    def advance(t, state):
        state = list(state)
        for b in range(batches):
            at = b * length + t
            s, u = step3[at], du3[at]
            y = None
            for n in range(nstate):
                k = b * nstate + n
                state[k] = jnp.exp2(s * rate[n]) * state[k] + u * bc[at * 2 * nstate + n]
                part = state[k] * bc[at * 2 * nstate + nstate + n]
                y = part if y is None else y + part
            y3[at] = y
        return tuple(state)

    state = tuple(start[b, n] for b in range(batches) for n in range(nstate))
    lax.fori_loop(0, length, advance, state, unroll=4)
    for j in range(y3.shape[1]):
        gate = z[:, j * 128 : (j + 1) * 128].astype(F32)
        gate = gate / (1.0 + jnp.exp(-gate))
        gated[:, j * 128 : (j + 1) * 128] = (y3[:, j, :] * gate).astype(BF)


def scaled_dot(j, order, deep, lhs, gain, head):
    values = lhs.astype(F32)
    at = pl.ds(pl.multiple_of(order[j] * deep, deep), deep)
    squares = jnp.sum(values * values, axis=-1, keepdims=True)
    return dot((values * gain[:, at]).astype(BF), head[...]), squares


def add_blocks(pieces, order, gain, head, before, acc, squares):
    deep = head.shape[0]
    per = pieces[0].shape[1] // deep
    for j in range(len(pieces) // 2 * per):

        @pl.when(pl.program_id(0) == j)
        def _():
            cut = slice(j % per * deep, (j % per + 1) * deep)
            upper, lower = pieces[j // per * 2 : j // per * 2 + 2]
            lhs = jnp.concatenate([upper[:, cut], lower[:, cut]], axis=0)
            product, part = scaled_dot(j, order, deep, lhs, gain, head)
            part = jnp.broadcast_to(part, squares.shape)
            if j > 0:
                acc[...] += product
                squares[...] += part
            elif before:
                acc[...] = product + before[0][...]
                squares[...] = part + before[1][...]
            else:
                acc[...] = product
                squares[...] = part


def own_kernel(order, upper, lower, gain, head, acc, squares):
    add_blocks((upper, lower), order, gain, head, None, acc, squares)


def near_kernel(order, a, b, c, d, gain, head, acc_in, squares_in, acc, squares):
    add_blocks((a, b, c, d), order, gain, head, (acc_in, squares_in), acc, squares)


def last_kernel(order, upper, lower, gain, head, acc_in, squares_in, ids, stats, acc, squares):
    add_blocks((upper, lower), order, gain, head, (acc_in, squares_in), acc, squares)
    per = upper.shape[1] // head.shape[0]
    width = gain.shape[1]

    @pl.when(pl.program_id(0) == per - 1)
    def _():
        rows, some = acc.shape[0], 16
        lane = lax.broadcasted_iota(jnp.int32, (some, 128), 1)
        entry = lax.broadcasted_iota(jnp.int32, (some, acc.shape[1]), 1)
        for r in range(0, rows, some):
            cut = slice(r, r + some)
            logits = acc[cut] * lax.rsqrt(squares[cut, :1] / width + 1e-05)
            top = jnp.max(logits, axis=-1, keepdims=True)
            exps = jnp.sum(jnp.exp(logits - top), axis=-1, keepdims=True)
            picked = jnp.sum(jnp.where(entry == ids[cut], logits, 0.0), axis=-1, keepdims=True)
            stats[cut] = jnp.where(lane == 0, top, jnp.where(lane == 1, exps, picked))


def pieces_kernel(lhs, *refs):
    at, total = 0, None
    for w in refs[:-1]:
        deep = w.shape[0]
        part = dot(lhs[:, at : at + deep], w[...])
        total = part if total is None else total + part
        at += deep
    refs[-1][...] = total.astype(refs[-1].dtype)


def finish_kernel(base, lengths, stats, token, sums):
    tops = [stats[k, 0:1] for k in range(stats.shape[0])]
    top = tops[0]
    for t in tops[1:]:
        top = jnp.maximum(top, t)
    exps = sum(stats[k, 1:2] * jnp.exp(t - top) for k, t in enumerate(tops))
    picked = sum(stats[k, 2:3] for k in range(stats.shape[0]))
    logp = picked - (top + jnp.log(exps))
    batches, length = token.shape
    position = base[0] + lax.broadcasted_iota(jnp.int32, (1, length), 1)
    total = jnp.zeros((1, 1), F32)
    for b in range(batches):
        part = logp[:, b * length : (b + 1) * length]
        token[b : b + 1] = part
        masked = jnp.where(position < lengths[b], part, 0.0)
        total = total + jnp.sum(masked, axis=1, keepdims=True)
    sums[...] = jnp.broadcast_to(total[None], sums.shape)


def vmem():
    return pl.BlockSpec(memory_space=pltpu.VMEM)


def smem():
    return pl.BlockSpec(memory_space=pltpu.SMEM)


def body(
    resid,
    norm_gain,
    in_x,
    in_z,
    conv_w,
    conv_b,
    xdt_w,
    xbc_w,
    dt_gain,
    dt_proj,
    dt_bias,
    a_rate,
    out_w,
    final_gain,
    head_w,
    targets,
    lengths,
):
    batch_count, local_len, width = resid.shape
    k_rows, channels = in_x.shape
    nstate = a_rate.shape[1]
    taps = conv_w.shape[0]
    rank = xdt_w.shape[1]
    rows = batch_count * local_len
    y, x, core = (lax.axis_index(a) for a in DP)
    zi = lax.axis_index("vocab")
    zs = lax.axis_size("vocab")

    order = [(i, i + 1) for i in range(YS * XS * CS - 1)]
    tail = lax.ppermute(resid[:, local_len - (taps - 1) :, :], DP, order)
    near = {s: lax.ppermute(in_x, DP, turns(s, 0)) for s in (1, 3, 2)}
    first = jnp.concatenate([in_x, near[1]], axis=0)
    second = jnp.concatenate([near[2], near[3]], axis=0)
    halo = 16
    tail = jnp.pad(
        tail.reshape(batch_count * (taps - 1), width),
        ((0, halo - batch_count * (taps - 1)), (0, 0)),
    )
    flat = resid.reshape(rows, width)
    half_rows = jax.ShapeDtypeStruct((rows + halo, width // CS), BF)
    normed, mine, theirs = pl.pallas_call(
        lambda *refs: norm_kernel(k_rows, *refs),
        out_shape=(jax.ShapeDtypeStruct((rows, width), BF), half_rows, half_rows),
        in_specs=[smem()] + [vmem()] * 3,
        out_specs=(vmem(),) * 3,
        scratch_shapes=[pltpu.VMEM((halo, width), BF)],
        compiler_params=pltpu.CompilerParams(vmem_limit_bytes=48 << 20),
        name="norm",
    )(
        jnp.stack(blocks_in_order(y, x, core) + blocks_in_order(y, x, 1 - core)),
        flat,
        tail,
        norm_gain.reshape(1, width),
    )
    first, second, mine, theirs, in_z = lax.optimization_barrier(
        (first, second, mine, theirs, in_z)
    )
    all_z = lax.all_gather(in_z, DP, axis=0, tiled=True)
    behind_first = lax.ppermute(first, DP, turns(1, 1))
    ahead_second = lax.ppermute(second, DP, turns(3, 1))
    behind_second = lax.ppermute(second, DP, turns(1, 1))
    ahead_first = lax.ppermute(first, DP, turns(3, 1))
    far_first = lax.ppermute(behind_first, DP, turns(1, 1))
    far_second = lax.ppermute(ahead_second, DP, turns(3, 1))
    share = width // zs
    out_cut = [
        lax.dynamic_slice_in_dim(out_w, lax.rem(zi + by, zs) * share, share, 1)
        for by in range(zs)
    ]
    far_first, far_second, out_cut = lax.optimization_barrier((far_first, far_second, out_cut))
    pieces = [
        first, second, behind_first, behind_second, far_first, far_second, ahead_first, ahead_second
    ]

    def half_dot(lhs, kind, name):
        return pl.pallas_call(
            pieces_kernel,
            out_shape=jax.ShapeDtypeStruct((lhs.shape[0], channels), kind),
            in_specs=[vmem()] * (1 + len(pieces)),
            out_specs=vmem(),
            compiler_params=pltpu.CompilerParams(vmem_limit_bytes=48 << 20),
            name=name,
        )(lhs, *pieces)

    theirs = swap_cores(theirs)
    from_them = swap_cores(half_dot(theirs, BF, "x_theirs"))
    x_acc = half_dot(mine, F32, "x_mine") + from_them.astype(F32)
    x_all = x_acc.astype(BF)
    x_inner = x_all[:rows].reshape(batch_count, local_len, channels)
    before = x_all[rows : rows + batch_count * (taps - 1)].reshape(batch_count, taps - 1, channels)
    padded = jnp.concatenate([before, x_inner], axis=1).astype(F32)
    conv_sum = jnp.zeros((batch_count, local_len, channels), F32) + conv_b
    for k in range(taps):
        conv_sum = conv_sum + conv_w[k] * padded[:, k : k + local_len, :]
    conv_act = jax.nn.silu(conv_sum).reshape(rows, channels)
    low = dot(conv_act.astype(BF), jnp.concatenate([xdt_w, xbc_w], axis=1))
    low_sent = low.astype(BF)
    low_sum = low_sent.astype(F32)
    for s in (1, 3, 2):
        low_sum = low_sum + lax.ppermute(low_sent, "vocab", ring(zs, s)).astype(F32)
    head_t, _, _ = lax.optimization_barrier((head_w.T, all_z, low_sum))
    all_head = lax.all_gather(head_t, DP, axis=0, tiled=True)
    dt_raw = low_sum[:, :rank]
    bc_raw = low_sum[:, rank:].reshape(-1)

    fold = channels // 128
    rate = (a_rate.T * (-LOG2E)).reshape(nstate, fold, 128)
    seq = jax.ShapeDtypeStruct((rows, fold, 128), F32)
    step3, du3, last, total = pl.pallas_call(
        lambda *refs: steps_kernel(rows, local_len, nstate, *refs),
        out_shape=(
            seq,
            seq,
            jax.ShapeDtypeStruct((batch_count, nstate, fold, 128), F32),
            jax.ShapeDtypeStruct((batch_count, fold, 128), F32),
        ),
        in_specs=[smem()] + [vmem()] * 6,
        out_specs=(vmem(),) * 4,
        compiler_params=pltpu.CompilerParams(vmem_limit_bytes=48 << 20),
        name="steps",
    )(
        bc_raw,
        dt_raw,
        dt_gain.reshape(1, rank),
        dt_proj,
        dt_bias.reshape(1, channels),
        conv_act,
        rate,
    )

    half = nstate // CS
    own = lax.dynamic_slice_in_dim(last, core * half, half, 1)
    other = lax.dynamic_slice_in_dim(last, (1 - core) * half, half, 1)
    rate_half = lax.dynamic_slice_in_dim(rate, core * half, half, 0)
    sent = jnp.concatenate([other, total[:, None]], axis=1)
    got = swap_cores(sent)
    state_0 = jnp.where(core == 0, own, got[:, :half])
    state_1 = jnp.where(core == 0, got[:, :half], own)
    total_0 = jnp.where(core == 0, total, got[:, half])
    total_1 = jnp.where(core == 0, got[:, half], total)

    def decay(steps):
        return jnp.exp2(steps[:, None] * rate_half)

    chip_state = decay(total_1) * state_0 + state_1
    chip_total = total_0 + total_1
    coarse = chip_total.astype(BF)
    fine = (chip_total - coarse.astype(F32)).astype(BF)
    packed = jnp.concatenate(
        [chip_state.astype(BF), coarse[:, None], fine[:, None]], axis=1
    )
    chips = YS * XS
    everyone = lax.all_to_all(
        jnp.broadcast_to(packed[None], (chips, *packed.shape)), CHIPS, 0, 0, tiled=True
    )
    z_gate = dot(normed, all_z).astype(BF)
    everyone, z_gate = lax.optimization_barrier((everyone, z_gate))
    chip = y * XS + x
    enter = jnp.zeros_like(chip_state)
    for k in range(chips - 1):
        part = everyone[k].astype(F32)
        later = decay(part[:, half] + part[:, half + 1]) * enter + part[:, :half]
        enter = jnp.where(k < chip, later, enter)
    enter_1 = decay(total_0) * enter + state_0
    kept = jnp.where(core == 0, enter, enter_1)
    given = swap_cores(jnp.where(core == 0, enter_1, enter))
    start = jnp.concatenate(
        [jnp.where(core == 0, kept, given), jnp.where(core == 0, given, kept)], axis=1
    )

    gated = pl.pallas_call(
        lambda *refs: outputs_kernel(rows, local_len, nstate, *refs),
        out_shape=jax.ShapeDtypeStruct((rows, channels), BF),
        in_specs=[smem()] + [vmem()] * 5,
        out_specs=vmem(),
        scratch_shapes=[pltpu.VMEM((rows, fold, 128), F32)],
        compiler_params=pltpu.CompilerParams(vmem_limit_bytes=48 << 20),
        name="outputs",
    )(bc_raw, step3, du3, rate, start, z_gate)

    def hops(by):
        return ring(zs, by)

    middle = rows // 2
    far = dot(gated, out_cut[2]).astype(BF)
    up = lax.ppermute(far[:middle], "vocab", hops(1))
    down = lax.ppermute(far[middle:], "vocab", hops(3))
    after = dot(gated, out_cut[1])
    prior = dot(gated, out_cut[3])
    part = lax.dynamic_slice_in_dim(flat, zi * share, share, 1).astype(F32)
    mixer = dot(gated, out_cut[0]) + part
    up, mixer = lax.optimization_barrier((up, mixer))
    up_low = lax.ppermute(after[middle:].astype(BF), "vocab", hops(1))
    down_high = lax.ppermute(prior[:middle].astype(BF), "vocab", hops(3))
    up_high = lax.ppermute(
        (after[:middle] + up.astype(F32)).astype(BF), "vocab", hops(1)
    )
    down_low = lax.ppermute(
        (prior[middle:] + down.astype(F32)).astype(BF), "vocab", hops(3)
    )
    upper = (mixer[:middle] + (up_high.astype(F32) + down_high.astype(F32))).astype(BF)
    lower = (mixer[middle:] + (up_low.astype(F32) + down_low.astype(F32))).astype(BF)
    hidden_share = jnp.concatenate([upper, lower], axis=0)

    behind_upper = lax.ppermute(upper, "vocab", hops(1))
    ahead_lower = lax.ppermute(lower, "vocab", hops(3))
    behind_lower = lax.ppermute(lower, "vocab", hops(1))
    ahead_upper = lax.ppermute(upper, "vocab", hops(3))
    opposite_upper = lax.ppermute(behind_upper, "vocab", hops(1))
    opposite_lower = lax.ppermute(ahead_lower, "vocab", hops(3))
    vocab_rows = head_w.shape[0]
    gain = final_gain.reshape(1, width)

    def blocks(per, *hops_back):
        firsts = [lax.rem(zi - s + zs, zs) * per for s in hops_back]
        return jnp.stack([first + i for first in firsts for i in range(per)])

    def whole(*shape):
        return vmem()

    sums = [whole(rows, vocab_rows), whole(rows, 128)]
    sums_shape = (
        jax.ShapeDtypeStruct((rows, vocab_rows), F32),
        jax.ShapeDtypeStruct((rows, 128), F32),
    )

    def logits_call(kernel, name, deep, from_where, pieces, extra, last=False):
        per = share // deep
        head_block = pl.BlockSpec((deep, vocab_rows), lambda j, order: (order[j], 0))
        halves = [whole(middle, share)] * len(pieces)
        weights = [whole(1, width), head_block]
        extra_specs = [whole(*e.shape) for e in extra]
        return pl.pallas_call(
            kernel,
            grid_spec=pltpu.PrefetchScalarGridSpec(
                num_scalar_prefetch=1,
                grid=(len(pieces) // 2 * per,),
                in_specs=halves + weights + extra_specs,
                out_specs=whole(rows, 128) if last else tuple(sums),
                scratch_shapes=[pltpu.VMEM(s.shape, F32) for s in sums_shape] if last else [],
            ),
            out_shape=jax.ShapeDtypeStruct((rows, 128), F32) if last else sums_shape,
            compiler_params=pltpu.CompilerParams(vmem_limit_bytes=48 << 20),
            name=name,
        )(blocks(per, *from_where), *pieces, gain, all_head, *extra)

    acc = logits_call(own_kernel, "own_logits", share // 2, (0,), (upper, lower), ())
    acc = logits_call(
        near_kernel,
        "near_logits",
        share,
        (1, 3),
        (behind_upper, behind_lower, ahead_upper, ahead_lower),
        acc,
    )
    local_ids = targets.reshape(rows, 1) - zi * vocab_rows
    stats = logits_call(
        last_kernel,
        "last_logits",
        share // 2,
        (2,),
        (opposite_upper, opposite_lower),
        (*acc, local_ids),
        True,
    )
    stats = stats[:, :3].T
    stats = lax.all_to_all(
        jnp.broadcast_to(stats[None], (zs, *stats.shape)), "vocab", 0, 0, tiled=True
    )
    peers = YS * XS * CS
    token_logp, sums = pl.pallas_call(
        finish_kernel,
        out_shape=(
            jax.ShapeDtypeStruct((batch_count, local_len), F32),
            jax.ShapeDtypeStruct((peers, 1, 128), F32),
        ),
        in_specs=[smem(), smem(), vmem()],
        out_specs=(vmem(),) * 2,
        name="finish",
    )((lax.axis_index(DP) * local_len).reshape(1), lengths, stats)
    sums = lax.all_to_all(sums, DP, 0, 0, tiled=True)[:, 0, 0]
    mean_logp = jnp.sum(sums) / jnp.sum(lengths.astype(F32))
    return (hidden_share.reshape(batch_count, local_len, share), token_logp, mean_logp)


def solution(mesh):
    split = Mesh(mesh.devices.reshape(YS, XS, CS, mesh.shape["vocab"]), (*DP, "vocab"))
    return jax.shard_map(
        body,
        mesh=split,
        in_specs=(
            P(None, DP, None),
            P(),
            P(DP, "vocab"),
            P(DP, "vocab"),
            P(None, "vocab"),
            P("vocab"),
            P("vocab", None),
            P("vocab", None),
            P(),
            P(None, "vocab"),
            P("vocab"),
            P("vocab", None),
            P("vocab", None),
            P(),
            P("vocab", DP),
            P(None, DP),
            P(),
        ),
        out_specs=(P(None, DP, "vocab"), P(None, DP), P()),
        check_vma=False,
    )
```
